32 devices in a mesh: grp: 4 (over z), blk: 8 (over y, x, core).
Axes of the slice: x: 2, y: 2, z: 4, core: 2. Of those that a mesh axis runs over, the one named last changes fastest.
Arguments:
- modes: bfloat16 [3, 256, 8, 32, 128], P(None, None, 'grp', 'blk'), may hold values from -6 to 6
- metric: float32 [3, 8, 32, 128], P(None, 'grp', 'blk'), may hold values from 0.5 to 2
- block_map: int32 [8, 32, 128], P('grp', 'blk'), may hold values from 0 to 15
- flags: int32 [8, 32, 128], P('grp', 'blk'), may hold values from 0 to 2
- region_scale: float32 [16], replicated, may hold values from 0.5 to 2
Outputs:
- tensor: float32 [8, 256, 256], P(None, 'grp', 'blk')
The draws below stay inside these ranges and needn't reach their ends.
All inputs are finite; a program needn't handle non-finite values.
Results may differ from the reference program's by a relative error of at most 0.0042.
Values may be sent and summed in bfloat16 or wider, within the bound.
No kernel may reach another device: no remote copies, remote signals or barrier semaphores. Data moves between devices by JAX's collectives and lax.ppermute only.
A program may use at most 64 MiB of HBM per device.

```python
import math
import jax
import jax.numpy as jnp
from jax import lax

M = 256
KS = 8
REGIONS = 16
NZ = 128
NX = 8
NY = 32


def set_ends(entries, rng, smallest, high):
    spot = [jax.random.randint(jax.random.fold_in(rng, axis), (), 0, length) for axis, length in enumerate(entries.shape)]
    main_axis = entries.shape.index(max(entries.shape))
    neighbour = spot[:main_axis] + [(spot[main_axis] + 1) % entries.shape[main_axis]] + spot[main_axis + 1:]
    return entries.at[tuple(spot)].set(smallest).at[tuple(neighbour)].set(high)


def levels(stream_key, dims, pieces, smallest, high):
    def one(dim, shards_of):
        steps = jax.random.uniform(jax.random.fold_in(jax.random.fold_in(stream_key, 6), dim), (shards_of,), jnp.float32, smallest / len(pieces), high / len(pieces))
        return jnp.repeat(jnp.exp(steps), dims[dim] // shards_of).reshape((-1,) + (1,) * (len(dims) - dim - 1))

    gain = one(*pieces[0])
    for cut in pieces[1:]:
        gain = gain * one(*cut)
    return gain


def normal_values(rng, extent, deviation, reach, pieces=(), kind=jnp.bfloat16):
    level = levels(rng, extent, pieces, -0.22, 0.18) if pieces else 1.0
    drawn = jax.random.normal(rng, extent, jnp.float32) * deviation * level
    return jnp.minimum(jnp.maximum(drawn, -reach), reach).astype(kind)


def setup_inputs(seed: int = 0) -> dict:
    key_list = jax.random.split(jax.random.key(seed), 6)
    return {
        "modes": normal_values(key_list[0], (3, M, NX, NY, NZ), 1.0, 6.0, ((2, 4), (3, 8))),
        "metric": jnp.clip(jnp.exp(math.log(2.0) - 1.3862944 * jax.random.uniform(key_list[1], (3, NX, NY, NZ), jnp.float32) ** levels(key_list[1], (3, NX, NY, NZ), ((1, 4), (2, 8)), -0.2, 0.2)), 0.5, 2.0),
        "block_map": set_ends(jax.random.randint(key_list[2], (NX, NY, NZ), 0, REGIONS), jax.random.fold_in(key_list[2], 1), 0, REGIONS - 1).astype(jnp.int32),
        "flags": set_ends(jax.random.randint(key_list[3], (NX, NY, NZ), 0, 3), jax.random.fold_in(key_list[3], 1), 0, 2).astype(jnp.int32),
        "region_scale": jnp.clip(jnp.exp(jax.random.uniform(key_list[4], (REGIONS,), jnp.float32, math.log(0.5), math.log(2.0))), 0.5, 2.0),
    }


def stencil(padded, metric):
    gx = 0.5 * (padded[:, :, 2:, 1:-1, 1:-1] - padded[:, :, :-2, 1:-1, 1:-1]) * metric[0]
    gy = 0.5 * (padded[:, :, 1:-1, 2:, 1:-1] - padded[:, :, 1:-1, :-2, 1:-1]) * metric[1]
    gz = 0.5 * (padded[:, :, 1:-1, 1:-1, 2:] - padded[:, :, 1:-1, 1:-1, :-2]) * metric[2]
    return jnp.stack([gx, gy, gz])


def weights(block_map, flags, region_scale, metric, norm):
    labels = jnp.arange(region_scale.shape[0], dtype=jnp.int32)[:, None, None, None]
    scale = jnp.sum(jnp.where(block_map[None] == labels, region_scale[:, None, None, None], jnp.float32(0.0)), axis=0)
    fluid = jnp.where(flags == 0, jnp.float32(1.0), jnp.where(flags == 1, jnp.float32(0.0), jnp.float32(0.5)))
    return scale * fluid * norm / (metric[0] * metric[1] * metric[2])


def reference(modes, metric, block_map, flags, region_scale):
    norm = float(NX * NY * NZ) ** -0.5
    slab = modes[:, :KS].astype(jnp.float32)
    padded = jnp.pad(slab, ((0, 0), (0, 0), (1, 1), (1, 1), (1, 1)))
    grads = stencil(padded, metric)
    weight = weights(block_map, flags, region_scale, metric, norm)
    results = []
    for k in range(KS):
        grad_k = grads[:, :, k]

        def row(xi, total):
            local = lax.dynamic_slice_in_dim(modes, xi, 1, 2).astype(jnp.float32)
            grad_row = lax.dynamic_slice_in_dim(grad_k, xi, 1, 2)
            weight_row = lax.dynamic_slice_in_dim(weight, xi, 1, 0)
            mixed = local[0][None] * grad_row[:, 0][:, None]
            mixed = mixed + local[1][None] * grad_row[:, 1][:, None]
            mixed = mixed + local[2][None] * grad_row[:, 2][:, None]
            tested = (weight_row[None, None] * mixed).astype(jnp.bfloat16)
            tested = lax.optimization_barrier(tested).astype(jnp.float32)
            return total + lax.dot_general(tested, local, (((0, 2, 3, 4), (0, 2, 3, 4)), ((), ())), precision=lax.Precision.HIGHEST)

        total = lax.fori_loop(0, NX, row, jnp.zeros((M, M), jnp.float32))
        results.append(total)
    return jnp.stack(results)
```

```python
import jax
import jax.numpy as jnp
import numpy as np
from jax import lax
from jax.experimental import pallas as pl
from jax.experimental.pallas import tpu as pltpu
from jax.sharding import PartitionSpec as P

KS = 8
LANES = 128
TILE = 64
F32 = jnp.float32
BF16 = jnp.bfloat16


def halving_masks(blocks):
    bits = [1 << b for b in range(1, blocks.bit_length() - 1)]
    turn = len(bits) // 2
    return [bits, bits[turn:] + bits[:turn]]


def block_order(blocks, me):
    masks = halving_masks(blocks)
    depth = blocks.bit_length() - 1
    table = np.zeros((2, blocks), np.int32)
    for odd in range(2):
        for p in range(blocks):
            top = p >> (depth - 1)
            pattern = top
            for t, mask in enumerate(masks[odd ^ top]):
                if (p >> (depth - 2 - t)) & 1:
                    pattern ^= mask
            table[odd, p] = pattern
    return me ^ jnp.where(me % 2 == 1, jnp.asarray(table[1]), jnp.asarray(table[0]))


def x_halo(slab):
    count = lax.axis_size("grp")
    up = [(i, i + 1) for i in range(count - 1)]
    down = [(i + 1, i) for i in range(count - 1)]
    return (
        lax.ppermute(slab[:, :, -1:], "grp", up),
        lax.ppermute(slab[:, :, :1], "grp", down),
    )


def y_halo(slab, odd):
    count = lax.axis_size("blk")
    first, last = slab[:, :, :, :1], slab[:, :, :, -1:]
    far = [(i, i + 1) for i in range(1, count - 1, 2)]
    near = [(i, i + 1) for i in range(0, count - 1, 2)]
    far_in = lax.ppermute(jnp.where(odd, last, first), "blk", far + [(b, a) for a, b in far])
    near_in = lax.ppermute(jnp.where(odd, first, last), "blk", near + [(b, a) for a, b in near])
    return jnp.where(odd, near_in, far_in), jnp.where(odd, far_in, near_in)


def weights(block_map, flags, region_scale, metric, norm):
    labels = jnp.arange(region_scale.shape[0], dtype=jnp.int32)[:, None, None, None]
    scale = jnp.sum(
        jnp.where(block_map[None] == labels, region_scale[:, None, None, None], jnp.float32(0.0)),
        axis=0,
    )
    fluid = jnp.where(
        flags == 0, jnp.float32(1.0), jnp.where(flags == 1, jnp.float32(0.0), jnp.float32(0.5))
    )
    return scale * fluid * norm / (metric[0] * metric[1] * metric[2])


def relay_kernel(order_ref, rows_ref, wide_ref, adv_ref, flat_ref):
    _, cells, count, _ = wide_ref.shape
    blocks = order_ref.shape[0]
    width = count // blocks
    flat_ref[...] = rows_ref[0].astype(F32)
    for r in range(cells):
        wide_ref[0, r] = flat_ref[pl.ds(r, count, stride=cells), :]
    for p in range(blocks):
        start = pl.multiple_of(order_ref[p] * width, width)
        for r in range(cells):
            part = wide_ref[0, r, pl.ds(start, width), :]
            adv_ref[p * width : (p + 1) * width, r * LANES : (r + 1) * LANES] = part.astype(BF16)


def relay(order, rows, count, cells):
    comps = rows.shape[0]
    return pl.pallas_call(
        relay_kernel,
        grid_spec=pltpu.PrefetchScalarGridSpec(
            num_scalar_prefetch=1,
            grid=(comps,),
            in_specs=[pl.BlockSpec((1, count * cells, LANES), lambda c, _: (c, 0, 0))],
            out_specs=[
                pl.BlockSpec((1, cells, count, LANES), lambda c, _: (c, 0, 0, 0)),
                pl.BlockSpec((count, cells * LANES), lambda c, _: (0, c)),
            ],
            scratch_shapes=[pltpu.VMEM((count * cells, LANES), F32)],
        ),
        out_shape=[
            jax.ShapeDtypeStruct((comps, cells, count, LANES), F32),
            jax.ShapeDtypeStruct((count, comps * cells * LANES), BF16),
        ],
        name="relay",
    )(order, rows)


def tensor_kernel(wide_ref, adv_ref, diff_ref, scale_ref, keep_ref, send_ref, grad_ref, t0_ref, t1_ref):
    comps, cells, count, _ = wide_ref.shape
    dims = diff_ref.shape[0]
    half = keep_ref.shape[1]
    for d in range(dims):
        for c in range(comps):
            for k in range(KS):
                grad_ref[(k * dims + d) * comps + c] = diff_ref[d, c * KS + k] * scale_ref[d]

    def build(k, t_ref):
        for r in range(cells):
            for i in range(0, count, TILE):
                a = [wide_ref[c, r, i : i + TILE, :] for c in range(comps)]
                for d in range(dims):
                    at = (k * dims + d) * comps
                    g = [grad_ref[at + c, pl.ds(r, 1), :] for c in range(comps)]
                    total = a[0] * g[0]
                    for c in range(1, comps):
                        total = total + a[c] * g[c]
                    col = (d * cells + r) * LANES
                    t_ref[i : i + TILE, col : col + LANES] = total.astype(BF16)

    def contract(k, t_ref):
        out = lax.dot_general(
            adv_ref[...], t_ref[...], (((1,), (1,)), ((), ())), preferred_element_type=F32
        )
        keep_ref[k] = out[:half]
        send_ref[k] = out[half:].astype(BF16)

    build(0, t0_ref)

    def step(n, carry):
        build(2 * n + 1, t1_ref)
        contract(2 * n, t0_ref)
        build(2 * n + 2, t0_ref)
        contract(2 * n + 1, t1_ref)
        return carry

    lax.fori_loop(0, KS // 2 - 1, step, 0)
    build(KS - 1, t1_ref)
    contract(KS - 2, t0_ref)
    contract(KS - 1, t1_ref)


def tensor_parts(wide, adv, diff, scale):
    comps, cells, count, _ = wide.shape
    half = count // 2
    depth = adv.shape[1]
    return pl.pallas_call(
        tensor_kernel,
        out_shape=[
            jax.ShapeDtypeStruct((KS, half, count), F32),
            jax.ShapeDtypeStruct((KS, half, count), BF16),
        ],
        scratch_shapes=[
            pltpu.VMEM((KS * comps * comps, cells, LANES), F32),
            pltpu.VMEM((count, depth), BF16),
            pltpu.VMEM((count, depth), BF16),
        ],
        name="tensor_parts",
    )(wide, adv, diff, scale)


def pack_kernel(me_ref, keep_ref, recv_ref, own_ref, *rest):
    sends, chunk_ref = rest[:-1], rest[-1]
    groups = len(sends) + 1
    width = keep_ref.shape[2] // groups
    fold = KS // own_ref.shape[0]
    me = me_ref[0]
    for row in range(own_ref.shape[0]):
        full = [
            keep_ref[row * fold + q] + recv_ref[row * fold + q].astype(F32) for q in range(fold)
        ]
        for z in range(groups):
            parts = [f[:, z * width : (z + 1) * width] for f in full]
            chunk_ref[me ^ z, row] = parts[0] if fold == 1 else jnp.concatenate(parts, axis=1)
    own_ref[...] = chunk_ref[0]
    for t, send in enumerate(sends):
        send[...] = chunk_ref[t + 1].astype(BF16)


def pack(me, keep, recv, groups):
    _, rows, count = keep.shape
    fold = max(1, LANES // (count // groups))
    shape = (KS // fold, rows, fold * count // groups)
    return pl.pallas_call(
        pack_kernel,
        in_specs=[
            pl.BlockSpec(memory_space=pltpu.SMEM),
            pl.BlockSpec(memory_space=pltpu.VMEM),
            pl.BlockSpec(memory_space=pltpu.VMEM),
        ],
        out_shape=[jax.ShapeDtypeStruct(shape, F32)]
        + [jax.ShapeDtypeStruct(shape, BF16)] * (groups - 1),
        scratch_shapes=[pltpu.VMEM((groups,) + shape, F32)],
        name="pack",
    )(me, keep, recv)


def finish_kernel(own_ref, *rest):
    recvs, out_ref = rest[:-1], rest[-1]
    fold = KS // own_ref.shape[0]
    width = out_ref.shape[1]
    for row in range(own_ref.shape[0]):
        total = own_ref[row]
        for recv in recvs:
            total = total + recv[row].astype(F32)
        turned = total.T
        for q in range(fold):
            out_ref[row * fold + q] = turned[q * width : (q + 1) * width, :]


def finish(own, recvs, width):
    rows = own.shape[1]
    return pl.pallas_call(
        finish_kernel,
        out_shape=jax.ShapeDtypeStruct((KS, width, rows), F32),
        name="finish",
    )(own, *recvs)


def local(modes, metric, block_map, flags, region_scale):
    groups = lax.axis_size("grp")
    blocks = lax.axis_size("blk")
    comps, count, nx, ny, nz = modes.shape
    cells = nx * ny
    total_cells = nx * groups * ny * blocks * nz
    norm = float(total_cells) ** (-0.5)
    me = lax.axis_index("blk")
    odd = me % 2 == 1

    slab = modes[:, :KS]
    x_prev, x_next = x_halo(slab)
    y_prev, y_next = y_halo(slab, odd)
    rows = modes.reshape(comps, count * cells, nz)
    wide, adv = relay(block_order(blocks, me), rows, count, cells)

    weight = weights(block_map, flags, region_scale, metric, norm)
    scale = (0.5 * metric * weight).reshape(comps, cells, nz)
    zero = jnp.zeros_like(slab[..., :1])

    def between(after, before):
        return after.astype(F32) - before.astype(F32)

    diff = jnp.stack(
        [
            between(
                jnp.concatenate([slab[:, :, 1:], x_next], 2),
                jnp.concatenate([x_prev, slab[:, :, :-1]], 2),
            ),
            between(
                jnp.concatenate([slab[:, :, :, 1:], y_next], 3),
                jnp.concatenate([y_prev, slab[:, :, :, :-1]], 3),
            ),
            between(
                jnp.concatenate([slab[..., 1:], zero], 4),
                jnp.concatenate([zero, slab[..., :-1]], 4),
            ),
        ]
    ).reshape(3, comps * KS, cells, nz)

    keep, send = tensor_parts(wide, adv, diff, scale)
    masks = halving_masks(blocks)
    steps = [[1, 1]] + [list(pair) for pair in zip(*masks)]
    for n, pair in enumerate(steps):
        recv = lax.ppermute(send, "blk", [(i, i ^ pair[i % 2]) for i in range(blocks)])
        if n + 1 < len(steps):
            total = keep + recv.astype(F32)
            half = total.shape[1] // 2
            keep, send = total[:, :half], total[:, half:].astype(BF16)

    own, *sends = pack(lax.axis_index("grp").reshape(1), keep, recv, groups)
    recvs = [
        lax.ppermute(sent, "grp", [(i, i ^ (t + 1)) for i in range(groups)])
        for t, sent in enumerate(sends)
    ]
    return finish(own, recvs, count // groups)


def solution(mesh):
    return jax.shard_map(
        local,
        mesh=mesh,
        in_specs=(
            P(None, None, "grp", "blk", None),
            P(None, "grp", "blk", None),
            P("grp", "blk", None),
            P("grp", "blk", None),
            P(),
        ),
        out_specs=P(None, "grp", "blk"),
        check_vma=False,
    )
```

```python
import jax
import jax.numpy as jnp
import numpy as np
from jax import lax
from jax.experimental import pallas as pl
from jax.experimental.pallas import tpu as pltpu
from jax.sharding import PartitionSpec as P

KS = 8
LANES = 128
TILE = 64
F32 = jnp.float32
BF16 = jnp.bfloat16


def halving_masks(devices, first):
    bits = [1 << b for b in range(first, devices.bit_length() - 1)]
    if first == 0 and len(bits) > 1:
        bits[1] |= 1
    turn = len(bits) // 2
    return [bits, bits[turn:] + bits[:turn]]


def xor_table(masks):
    table = [0]
    for mask in reversed(masks):
        table = table + [t ^ mask for t in table]
    return table


def adv_order(blocks, me, odd):
    even_masks, odd_masks = halving_masks(blocks, 1)
    near, far = xor_table(even_masks), xor_table(odd_masks)
    tables = jnp.asarray([near + [t ^ 1 for t in far], far + [t ^ 1 for t in near]], jnp.int32)
    return me ^ jnp.where(odd, tables[1], tables[0])


def test_order(groups, me, odd):
    tables = jnp.asarray([xor_table(m) for m in halving_masks(groups, 0)], jnp.int32)
    return me ^ jnp.where(odd, tables[1], tables[0])


def vmem(shape, dtype):
    return pltpu.VMEM(shape, dtype)


def inside(x):
    return pltpu.with_memory_space_constraint(x, pltpu.VMEM)


def relay_kernel(order_ref, region_ref, rows_ref, metric_ref, map_ref, flag_ref, norm, wide_ref, adv_ref,
                 scale_ref, in_ref, flat_ref, sem):
    comps, cells, count, _ = wide_ref.shape
    blocks = order_ref.shape[0]
    width = count // blocks
    copies = [
        pltpu.make_async_copy(rows_ref.at[c], in_ref.at[c], sem.at[c]) for c in range(comps)
    ]
    for copy in copies:
        copy.start()
    scale = jnp.zeros(map_ref.shape, F32)
    for label in range(region_ref.shape[0]):
        scale = jnp.where(map_ref[...] == label, region_ref[label], scale)
    flags = flag_ref[...]
    fluid = jnp.where(flags == 0, 1.0, jnp.where(flags == 1, 0.0, 0.5))
    weight = scale * fluid * norm / (metric_ref[0] * metric_ref[1] * metric_ref[2])
    for d in range(comps):
        scale_ref[d] = 0.5 * metric_ref[d] * weight
    for c in range(comps):
        copies[c].wait()
        flat_ref[c] = in_ref[c].astype(F32)
        for r in range(cells):
            wide_ref[c, r] = flat_ref[c, pl.ds(r, count, stride=cells), :]
        for p in range(blocks):
            start = pl.multiple_of(order_ref[p] * width, width)
            for r in range(cells):
                part = wide_ref[c, r, pl.ds(start, width), :]
                col = (c * cells + r) * LANES
                adv_ref[p * width : (p + 1) * width, col : col + LANES] = part.astype(BF16)


def relay(order, region_scale, rows, metric, block_map, flags, norm, count):
    comps, total, _ = rows.shape
    cells = total // count
    smem = pl.BlockSpec(memory_space=pltpu.SMEM)
    whole = pl.BlockSpec(memory_space=pltpu.VMEM)
    return pl.pallas_call(
        lambda *refs: relay_kernel(*refs[:6], norm, *refs[6:]),
        in_specs=[smem, smem, pl.BlockSpec(memory_space=pl.ANY), whole, whole, whole],
        out_shape=[
            vmem((comps, cells, count, LANES), F32),
            vmem((count, comps * cells * LANES), BF16),
            vmem((comps, cells, LANES), F32),
        ],
        scratch_shapes=[
            pltpu.VMEM((comps, total, LANES), BF16),
            pltpu.VMEM((comps, total, LANES), F32),
            pltpu.SemaphoreType.DMA((comps,)),
        ],
        compiler_params=pltpu.CompilerParams(vmem_limit_bytes=16 << 20),
        name="relay",
    )(order, region_scale, rows, metric, block_map, flags)


def tensor_kernel(order_ref, edge_ref, wide_ref, adv_ref, scale_ref, slab_ref, down_ref, up_ref, near_ref,
                  far_ref, swap, ny, keep_ref, send_ref, grad_ref, t0_ref, t1_ref):
    comps, cells, count, _ = wide_ref.shape
    half = keep_ref.shape[1]
    chunks = order_ref.shape[0]
    width = count // chunks
    tile = min(width, TILE)
    odd = edge_ref[4] == 1
    row = lax.broadcasted_iota(jnp.int32, (cells, LANES), 0)
    lane = lax.broadcasted_iota(jnp.int32, (cells, LANES), 1)
    ends = [edge_ref[e] == 1 for e in range(4)]

    def shift_in(own, before, after, by, axis, first, last, no_before, no_after):
        size = own.shape[axis]
        prev = pltpu.roll(own, by, axis)
        succ = pltpu.roll(own, size - by, axis)
        if before is not None:
            before = jnp.where(no_before, 0.0, pltpu.roll(before, first[1], 0) if first[1] else before)
            after = jnp.where(no_after, 0.0, pltpu.roll(after, last[1], 0) if last[1] else after)
        else:
            before = after = 0.0
        return jnp.where(last[0], after, succ) - jnp.where(first[0], before, prev)

    for c in range(comps):
        for k in range(KS):
            at = pl.ds(k * cells, cells)
            own, down, up, near, far = (
                ref[c, at, :].astype(F32) for ref in (slab_ref, down_ref, up_ref, near_ref, far_ref)
            )
            left, right = jnp.where(odd, near, far), jnp.where(odd, far, near)
            shift_x = ny % cells
            diffs = [
                shift_in(own, down, up, ny % cells, 0, (row < ny, shift_x), (row >= cells - ny, shift_x),
                         ends[0], ends[1]),
                shift_in(own, left, right, 1, 0, (row % ny == 0, (cells - ny + 1) % cells),
                         (row % ny == ny - 1, (ny - 1) % cells), ends[2], ends[3]),
                shift_in(own, None, None, 1, 1, (lane == 0, 0), (lane == LANES - 1, 0), None, None),
            ]
            for d in range(comps):
                grad_ref[(k * comps + d) * comps + c] = diffs[d] * scale_ref[d]

    def build(k, t_ref):
        for q in range(chunks):
            base = pl.multiple_of(order_ref[q] * width, width)
            for r in range(cells):
                for i in range(0, width, tile):
                    a = [wide_ref[c, r, pl.ds(base + i, tile), :] for c in range(comps)]
                    for d in range(comps):
                        at = (k * comps + d) * comps
                        g = [grad_ref[at + c, pl.ds(r, 1), :] for c in range(comps)]
                        total = a[0] * g[0]
                        for c in range(1, comps):
                            total = total + a[c] * g[c]
                        col = (d * cells + r) * LANES
                        top = q * width + i
                        t_ref[top : top + tile, col : col + LANES] = total.astype(BF16)

    def contract(k, t_ref):
        out = lax.dot_general(
            adv_ref[...], t_ref[...], (((1,), (1,)), ((), ())), preferred_element_type=F32
        )
        keep_ref[k] = out[:half]
        gone = out[half:]
        send_ref[k] = jnp.concatenate(
            [gone[:, s * width : (s + 1) * width] for s in swap], axis=1
        ).astype(BF16)

    build(0, t0_ref)

    def step(n, carry):
        build(2 * n + 1, t1_ref)
        contract(2 * n, t0_ref)
        build(2 * n + 2, t0_ref)
        contract(2 * n + 1, t1_ref)
        return carry

    lax.fori_loop(0, KS // 2 - 1, step, 0)
    build(KS - 1, t1_ref)
    contract(KS - 2, t0_ref)
    contract(KS - 1, t1_ref)


def tensor_parts(order, edges, wide, adv, scale, slabs, swap, ny):
    comps, cells, count, _ = wide.shape
    half = count // 2
    depth = adv.shape[1]
    smem = pl.BlockSpec(memory_space=pltpu.SMEM)
    whole = pl.BlockSpec(memory_space=pltpu.VMEM)
    return pl.pallas_call(
        lambda *refs: tensor_kernel(*refs[:10], swap, ny, *refs[10:]),
        in_specs=[smem, smem] + [whole] * 8,
        out_shape=[vmem((KS, half, count), F32), vmem((KS, half, count), BF16)],
        scratch_shapes=[
            pltpu.VMEM((KS * comps * comps, cells, LANES), F32),
            pltpu.VMEM((count, depth), BF16),
            pltpu.VMEM((count, depth), BF16),
        ],
        compiler_params=pltpu.CompilerParams(vmem_limit_bytes=16 << 20),
        name="tensor_parts",
    )(order, edges, *(inside(x) for x in (wide, adv, scale, *slabs)))


def fold_parts(rows, group, side):
    half = group // 2
    first = side * half
    parts = [r[:, g + first : g + first + half] for r in rows for g in range(0, rows[0].shape[1], group)]
    return parts[0] if len(parts) == 1 else jnp.concatenate(parts, axis=1)


def fold(keep, recv, group):
    count, rows, lanes = keep.shape
    shape = (count // 2, rows, lanes)

    def kernel(keep_ref, recv_ref, own_ref, send_ref):
        for n in range(count // 2):
            pair = [keep_ref[m] + recv_ref[m].astype(F32) for m in (2 * n, 2 * n + 1)]
            own_ref[n] = fold_parts(pair, group, 0)
            send_ref[n] = fold_parts(pair, group, 1).astype(BF16)

    return pl.pallas_call(
        kernel,
        out_shape=[vmem(shape, F32), vmem(shape, BF16)],
        compiler_params=pltpu.CompilerParams(vmem_limit_bytes=4 << 20),
        name="fold",
    )(inside(keep), inside(recv))


def finish(keep, recv, width):
    count, rows, lanes = keep.shape
    pieces = lanes // width

    def kernel(keep_ref, recv_ref, out_ref):
        for n in range(count):
            total = keep_ref[n] + recv_ref[n].astype(F32)
            for q in range(pieces):
                out_ref[n * pieces + q] = total[:, q * width : (q + 1) * width]

    return pl.pallas_call(
        kernel,
        out_shape=jax.ShapeDtypeStruct((KS, rows, width), F32),
        compiler_params=pltpu.CompilerParams(vmem_limit_bytes=4 << 20),
        name="finish",
    )(inside(keep), inside(recv))


def exchange(send, axis, masks):
    count = lax.axis_size(axis)
    return lax.ppermute(send, axis, [(i, i ^ masks[i % 2]) for i in range(count)])


def local(modes, metric, block_map, flags, region_scale):
    groups = lax.axis_size("grp")
    blocks = lax.axis_size("blk")
    comps, count, nx, ny, nz = modes.shape
    cells = nx * ny
    total_cells = nx * groups * ny * blocks * nz
    norm = float(total_cells) ** (-0.5)
    block, layer = lax.axis_index("blk"), lax.axis_index("grp")
    odd = block % 2 == 1

    rows = modes.reshape(comps, count * cells, nz)
    slab = rows[:, : KS * cells]
    ring = range(groups)
    down = lax.ppermute(slab, "grp", [(i, (i + 1) % groups) for i in ring])
    up = lax.ppermute(slab, "grp", [((i + 1) % groups, i) for i in ring])
    turn = [(i + 1) % blocks if i % 2 else (i - 1) % blocks for i in range(blocks)]
    far = lax.ppermute(slab, "blk", list(enumerate(turn)))
    near = lax.ppermute(slab, "blk", [(i, i ^ 1) for i in range(blocks)])

    wide, adv, scale = relay(
        adv_order(blocks, block, odd),
        region_scale,
        rows,
        metric.reshape(comps, cells, nz),
        block_map.reshape(cells, nz),
        flags.reshape(cells, nz),
        norm,
        count,
    )
    edges = jnp.stack([layer == 0, layer == groups - 1, block == 0, block == blocks - 1, odd])
    even_masks, odd_masks = halving_masks(groups, 0)
    even_order = xor_table(even_masks)
    swap = [even_order.index(t) for t in xor_table(odd_masks)]
    keep, send = tensor_parts(
        test_order(groups, layer, odd),
        edges.astype(jnp.int32),
        wide,
        adv,
        scale,
        (slab, down, up, near, far),
        swap,
        ny,
    )

    recv = exchange(send, "blk", [1, 1])
    for masks in zip(*halving_masks(blocks, 1)):
        total = keep + recv.astype(F32)
        half = total.shape[1] // 2
        keep, send = total[:, :half], total[:, half:].astype(BF16)
        recv = exchange(send, "blk", masks)
    width = count
    for masks in zip(even_masks, odd_masks):
        if width > LANES:
            total = keep + recv.astype(F32)
            half = width // 2
            keep, send = total[..., :half], total[..., half:].astype(BF16)
        else:
            keep, send = fold(keep, recv, width)
        width //= 2
        pairs = [
            (g * blocks + b, (g ^ masks[b % 2]) * blocks + b)
            for g in range(groups)
            for b in range(blocks)
        ]
        recv = lax.ppermute(send, ("grp", "blk"), pairs)
    return jnp.swapaxes(finish(keep, recv, width), 1, 2)


def solution(mesh):
    return jax.shard_map(
        local,
        mesh=mesh,
        in_specs=(
            P(None, None, "grp", "blk", None),
            P(None, "grp", "blk", None),
            P("grp", "blk", None),
            P("grp", "blk", None),
            P(),
        ),
        out_specs=P(None, "grp", "blk"),
        check_vma=False,
    )
```

```python
import jax
import jax.numpy as jnp
import numpy as np
from jax import lax
from jax.experimental import pallas as pl
from jax.experimental.pallas import tpu as pltpu
from jax.sharding import PartitionSpec as P

KS = 8
LANES = 128
TILE = 64
F32 = jnp.float32
BF16 = jnp.bfloat16


def halving_masks(devices, first):
    bits = [1 << b for b in range(first, devices.bit_length() - 1)]
    turn = len(bits) // 2
    return [bits, bits[turn:] + bits[:turn]]


def xor_table(masks):
    table = [0]
    for mask in reversed(masks):
        table = table + [t ^ mask for t in table]
    return table


def place():
    block, layer = lax.axis_index("blk"), lax.axis_index("grp")
    return block, layer, block % 2 == 1


def adv_order(blocks):
    block, _, odd = place()
    near, far = (xor_table(masks) for masks in halving_masks(blocks, 1))
    even = near + [t ^ 1 for t in far]
    other = far + [t ^ 1 for t in near]
    return [block ^ (e if e == o else jnp.where(odd, o, e)) for e, o in zip(even, other)]


def test_order(groups):
    _, layer, odd = place()
    even, other = (xor_table(masks) for masks in halving_masks(groups, 0))
    return [layer ^ (e if e == o else jnp.where(odd, o, e)) for e, o in zip(even, other)]


def vmem(shape, dtype):
    return pltpu.VMEM(shape, dtype)


def inside(x):
    return pltpu.with_memory_space_constraint(x, pltpu.VMEM)


def relay_kernel(region_in, rows_in, metric_in, map_in, flag_in, norm, blocks, wide_ref, adv_ref,
                 scale_ref, region_ref, rows_ref, metric_ref, map_ref, flag_ref, flat_ref, sem):
    comps, cells, count, _ = wide_ref.shape
    width = count // blocks
    pairs = [(region_in, region_ref), (metric_in, metric_ref), (map_in, map_ref), (flag_in, flag_ref)]
    pairs += [(rows_in.at[c], rows_ref.at[c]) for c in range(comps)]
    copies = [pltpu.make_async_copy(a, b, sem.at[n]) for n, (a, b) in enumerate(pairs)]
    for copy in copies[4:] + copies[:4]:
        copy.start()
    order = adv_order(blocks)
    for c in range(comps):
        copies[4 + c].wait()
        flat_ref[c] = rows_ref[c].astype(F32)
        for r in range(cells):
            wide_ref[c, r] = flat_ref[c, pl.ds(r, count, stride=cells), :]
        for p in range(blocks):
            start = pl.multiple_of(order[p] * width, width)
            for r in range(cells):
                part = wide_ref[c, r, pl.ds(start, width), :]
                adv_ref[c * cells + r, p * width : (p + 1) * width, :] = part.astype(BF16)
    for copy in copies[:4]:
        copy.wait()
    scale = jnp.zeros(map_ref.shape, F32)
    for label in range(region_ref.shape[0]):
        scale = jnp.where(map_ref[...] == label, region_ref[label], scale)
    flags = flag_ref[...]
    fluid = jnp.where(flags == 0, 1.0, jnp.where(flags == 1, 0.0, 0.5))
    weight = scale * fluid * norm / (metric_ref[0] * metric_ref[1] * metric_ref[2])
    for d in range(comps):
        scale_ref[d] = 0.5 * metric_ref[d] * weight


def relay(region_scale, rows, metric, block_map, flags, norm, count, blocks):
    comps, total, _ = rows.shape
    cells = total // count
    return pl.pallas_call(
        lambda *refs: relay_kernel(*refs[:5], norm, blocks, *refs[5:]),
        in_specs=[pl.BlockSpec(memory_space=pltpu.HBM)] * 5,
        out_shape=[
            vmem((comps, cells, count, LANES), F32),
            vmem((comps * cells, count, LANES), BF16),
            vmem((comps, cells, LANES), F32),
        ],
        scratch_shapes=[
            pltpu.SMEM(region_scale.shape, F32),
            pltpu.VMEM(rows.shape, BF16),
            pltpu.VMEM(metric.shape, F32),
            pltpu.VMEM(block_map.shape, jnp.int32),
            pltpu.VMEM(flags.shape, jnp.int32),
            pltpu.VMEM((comps, total, LANES), F32),
            pltpu.SemaphoreType.DMA((4 + comps,)),
        ],
        compiler_params=pltpu.CompilerParams(vmem_limit_bytes=16 << 20),
        name="relay",
    )(*(
        pltpu.with_memory_space_constraint(x, pltpu.HBM)
        for x in (region_scale, rows, metric, block_map, flags)
    ))


def tensor_kernel(wide_ref, adv_ref, scale_ref, slab_ref, down_ref, up_ref, near_ref,
                  far_ref, swap, ny, groups, blocks, keep_ref, send_ref, grad_ref, t0_ref, t1_ref):
    comps, cells, count, _ = wide_ref.shape
    half = keep_ref.shape[1]
    width = count // groups
    tile = min(width, TILE)
    order = test_order(groups)
    block, layer, odd = place()
    row = lax.broadcasted_iota(jnp.int32, (cells, LANES), 0)
    lane = lax.broadcasted_iota(jnp.int32, (cells, LANES), 1)
    ends = [layer == 0, layer == groups - 1, block == 0, block == blocks - 1]

    def shift_in(own, before, after, by, axis, first, last, no_before, no_after):
        size = own.shape[axis]
        prev = pltpu.roll(own, by, axis)
        succ = pltpu.roll(own, size - by, axis)
        if before is not None:
            before = jnp.where(no_before, 0.0, pltpu.roll(before, first[1], 0) if first[1] else before)
            after = jnp.where(no_after, 0.0, pltpu.roll(after, last[1], 0) if last[1] else after)
        else:
            before = after = 0.0
        return jnp.where(last[0], after, succ) - jnp.where(first[0], before, prev)

    for c in range(comps):
        for k in range(KS):
            at = pl.ds(k * cells, cells)
            own, down, up, near, far = (
                ref[c, at, :].astype(F32) for ref in (slab_ref, down_ref, up_ref, near_ref, far_ref)
            )
            left, right = jnp.where(odd, near, far), jnp.where(odd, far, near)
            shift_x = ny % cells
            diffs = [
                shift_in(own, down, up, ny % cells, 0, (row < ny, shift_x), (row >= cells - ny, shift_x),
                         ends[0], ends[1]),
                shift_in(own, left, right, 1, 0, (row % ny == 0, (cells - ny + 1) % cells),
                         (row % ny == ny - 1, (ny - 1) % cells), ends[2], ends[3]),
                shift_in(own, None, None, 1, 1, (lane == 0, 0), (lane == LANES - 1, 0), None, None),
            ]
            for d in range(comps):
                grad_ref[(k * comps + d) * comps + c] = diffs[d] * scale_ref[d]

    def build(k, t_ref):
        for q in range(groups):
            base = pl.multiple_of(order[q] * width, width)
            for r in range(cells):
                for i in range(0, width, tile):
                    a = [wide_ref[c, r, pl.ds(base + i, tile), :] for c in range(comps)]
                    for d in range(comps):
                        at = (k * comps + d) * comps
                        g = [grad_ref[at + c, pl.ds(r, 1), :] for c in range(comps)]
                        total = a[0] * g[0]
                        for c in range(1, comps):
                            total = total + a[c] * g[c]
                        top = q * width + i
                        t_ref[d * cells + r, top : top + tile, :] = total.astype(BF16)

    def contract(k, t_ref):
        adv, tested = (
            jnp.concatenate([ref[n] for n in range(ref.shape[0])], axis=1) for ref in (adv_ref, t_ref)
        )
        out = lax.dot_general(
            adv, tested, (((1,), (1,)), ((), ())), preferred_element_type=F32
        )
        keep_ref[k] = out[:half]
        gone = out[half:]
        send_ref[k] = jnp.concatenate(
            [gone[:, s * width : (s + 1) * width] for s in swap], axis=1
        ).astype(BF16)

    build(0, t0_ref)

    def step(n, carry):
        build(2 * n + 1, t1_ref)
        contract(2 * n, t0_ref)
        build(2 * n + 2, t0_ref)
        contract(2 * n + 1, t1_ref)
        return carry

    lax.fori_loop(0, KS // 2 - 1, step, 0)
    build(KS - 1, t1_ref)
    contract(KS - 2, t0_ref)
    contract(KS - 1, t1_ref)


def tensor_parts(wide, adv, scale, slabs, swap, ny, groups, blocks):
    comps, cells, count, _ = wide.shape
    half = count // 2
    return pl.pallas_call(
        lambda *refs: tensor_kernel(*refs[:8], swap, ny, groups, blocks, *refs[8:]),
        out_shape=[vmem((KS, half, count), F32), vmem((KS, half, count), BF16)],
        scratch_shapes=[
            pltpu.VMEM((KS * comps * comps, cells, LANES), F32),
            pltpu.VMEM(adv.shape, BF16),
            pltpu.VMEM(adv.shape, BF16),
        ],
        compiler_params=pltpu.CompilerParams(vmem_limit_bytes=16 << 20),
        name="tensor_parts",
    )(*(inside(x) for x in (wide, adv, scale, *slabs)))


def fold_parts(rows, group, side):
    half = group // 2
    first = side * half
    parts = [r[:, g + first : g + first + half] for r in rows for g in range(0, rows[0].shape[1], group)]
    return parts[0] if len(parts) == 1 else jnp.concatenate(parts, axis=1)


def fold(keep, recv, group):
    count, rows, lanes = keep.shape
    shape = (count // 2, rows, lanes)

    def kernel(keep_ref, recv_ref, own_ref, send_ref):
        for n in range(count // 2):
            pair = [keep_ref[m] + recv_ref[m].astype(F32) for m in (2 * n, 2 * n + 1)]
            own_ref[n] = fold_parts(pair, group, 0)
            send_ref[n] = fold_parts(pair, group, 1).astype(BF16)

    return pl.pallas_call(
        kernel,
        out_shape=[vmem(shape, F32), vmem(shape, BF16)],
        compiler_params=pltpu.CompilerParams(vmem_limit_bytes=4 << 20),
        name="fold",
    )(inside(keep), inside(recv))


def finish(keep, recv, width):
    count, rows, lanes = keep.shape
    pieces = lanes // width

    def kernel(keep_ref, recv_ref, out_ref):
        for n in range(count):
            total = keep_ref[n] + recv_ref[n].astype(F32)
            for q in range(pieces):
                out_ref[n * pieces + q] = total[:, q * width : (q + 1) * width]

    return pl.pallas_call(
        kernel,
        out_shape=jax.ShapeDtypeStruct((KS, rows, width), F32),
        compiler_params=pltpu.CompilerParams(vmem_limit_bytes=4 << 20),
        name="finish",
    )(inside(keep), inside(recv))


def exchange(send, axis, masks):
    count = lax.axis_size(axis)
    return lax.ppermute(send, axis, [(i, i ^ masks[i % 2]) for i in range(count)])


def local(modes, metric, block_map, flags, region_scale):
    groups = lax.axis_size("grp")
    blocks = lax.axis_size("blk")
    comps, count, nx, ny, nz = modes.shape
    cells = nx * ny
    total_cells = nx * groups * ny * blocks * nz
    norm = float(total_cells) ** (-0.5)

    rows = modes.reshape(comps, count * cells, nz)
    slab = rows[:, : KS * cells]
    ring = range(groups)
    down = lax.ppermute(slab, "grp", [(i, (i + 1) % groups) for i in ring])
    up = lax.ppermute(slab, "grp", [((i + 1) % groups, i) for i in ring])
    turn = [(i + 1) % blocks if i % 2 else (i - 1) % blocks for i in range(blocks)]
    far = lax.ppermute(slab, "blk", list(enumerate(turn)))
    near = lax.ppermute(slab, "blk", [(i, i ^ 1) for i in range(blocks)])

    wide, adv, scale = relay(
        region_scale,
        rows,
        metric.reshape(comps, cells, nz),
        block_map.reshape(cells, nz),
        flags.reshape(cells, nz),
        norm,
        count,
        blocks,
    )
    even_masks, odd_masks = halving_masks(groups, 0)
    even_order = xor_table(even_masks)
    swap = [even_order.index(t) for t in xor_table(odd_masks)]
    keep, send = tensor_parts(
        wide,
        adv,
        scale,
        (slab, down, up, near, far),
        swap,
        ny,
        groups,
        blocks,
    )

    recv = exchange(send, "blk", [1, 1])
    for masks in zip(*halving_masks(blocks, 1)):
        total = keep + recv.astype(F32)
        half = total.shape[1] // 2
        keep, send = total[:, :half], total[:, half:].astype(BF16)
        recv = exchange(send, "blk", masks)
    width = count
    for masks in zip(even_masks, odd_masks):
        if width > LANES:
            total = keep + recv.astype(F32)
            half = width // 2
            keep, send = total[..., :half], total[..., half:].astype(BF16)
        else:
            keep, send = fold(keep, recv, width)
        width //= 2
        pairs = [
            (g * blocks + b, (g ^ masks[b % 2]) * blocks + b)
            for g in range(groups)
            for b in range(blocks)
        ]
        recv = lax.ppermute(send, ("grp", "blk"), pairs)
    return jnp.swapaxes(finish(keep, recv, width), 1, 2)


def solution(mesh):
    return jax.shard_map(
        local,
        mesh=mesh,
        in_specs=(
            P(None, None, "grp", "blk", None),
            P(None, "grp", "blk", None),
            P("grp", "blk", None),
            P("grp", "blk", None),
            P(),
        ),
        out_specs=P(None, "grp", "blk"),
        check_vma=False,
    )
```

```python
import jax
import jax.numpy as jnp
import numpy as np
from jax import lax
from jax.experimental import pallas as pl
from jax.experimental.pallas import tpu as pltpu
from jax.sharding import PartitionSpec as P

KS = 8
LANES = 128
TILE = 64
F32 = jnp.float32
BF16 = jnp.bfloat16


def halving_masks(devices, first):
    bits = [1 << b for b in range(first, devices.bit_length() - 1)]
    turn = len(bits) // 2
    return [bits, bits[turn:] + bits[:turn]]


def xor_table(masks):
    table = [0]
    for mask in reversed(masks):
        table = table + [t ^ mask for t in table]
    return table


def place():
    block, layer = lax.axis_index("blk"), lax.axis_index("grp")
    return block, layer, block % 2 == 1


def adv_order(blocks):
    block, _, odd = place()
    near, far = (xor_table(masks) for masks in halving_masks(blocks, 1))
    even = near + [t ^ 1 for t in far]
    other = far + [t ^ 1 for t in near]
    return [block ^ (e if e == o else jnp.where(odd, o, e)) for e, o in zip(even, other)]


def test_order(groups):
    _, layer, odd = place()
    even, other = (xor_table(masks) for masks in halving_masks(groups, 0))
    return [layer ^ (e if e == o else jnp.where(odd, o, e)) for e, o in zip(even, other)]


def vmem(shape, dtype):
    return pltpu.VMEM(shape, dtype)


def inside(x):
    return pltpu.with_memory_space_constraint(x, pltpu.VMEM)


def relay_kernel(region_in, rows_in, metric_in, map_in, flag_in, norm, blocks, wide_ref, adv_ref,
                 scale_ref, region_ref, rows_ref, metric_ref, map_ref, flag_ref, flat_ref, sem):
    comps, cells, count, _ = wide_ref.shape
    width = count // blocks
    pairs = [(region_in, region_ref), (metric_in, metric_ref), (map_in, map_ref), (flag_in, flag_ref)]
    pairs += [(rows_in.at[c], rows_ref.at[c]) for c in range(comps)]
    copies = [pltpu.make_async_copy(a, b, sem.at[n]) for n, (a, b) in enumerate(pairs)]
    for copy in copies[4:] + copies[:4]:
        copy.start()
    order = adv_order(blocks)
    for c in range(comps):
        copies[4 + c].wait()
        flat_ref[c] = rows_ref[c].astype(F32)
        for r in range(cells):
            wide_ref[c, r] = flat_ref[c, pl.ds(r, count, stride=cells), :]
        for p in range(blocks):
            start = pl.multiple_of(order[p] * width, width)
            for r in range(cells):
                part = wide_ref[c, r, pl.ds(start, width), :]
                adv_ref[c * cells + r, p * width : (p + 1) * width, :] = part.astype(BF16)
    for copy in copies[:4]:
        copy.wait()
    scale = jnp.zeros(map_ref.shape, F32)
    for label in range(region_ref.shape[0]):
        scale = jnp.where(map_ref[...] == label, region_ref[label], scale)
    flags = flag_ref[...]
    fluid = jnp.where(flags == 0, 1.0, jnp.where(flags == 1, 0.0, 0.5))
    weight = scale * fluid * norm / (metric_ref[0] * metric_ref[1] * metric_ref[2])
    for d in range(comps):
        scale_ref[d] = 0.5 * metric_ref[d] * weight


def relay(region_scale, rows, metric, block_map, flags, norm, count, blocks):
    comps, total, _ = rows.shape
    cells = total // count
    return pl.pallas_call(
        lambda *refs: relay_kernel(*refs[:5], norm, blocks, *refs[5:]),
        in_specs=[pl.BlockSpec(memory_space=pltpu.HBM)] * 5,
        out_shape=[
            vmem((comps, cells, count, LANES), F32),
            vmem((comps * cells, count, LANES), BF16),
            vmem((comps, cells, LANES), F32),
        ],
        scratch_shapes=[
            pltpu.SMEM(region_scale.shape, F32),
            pltpu.VMEM(rows.shape, BF16),
            pltpu.VMEM(metric.shape, F32),
            pltpu.VMEM(block_map.shape, jnp.int32),
            pltpu.VMEM(flags.shape, jnp.int32),
            pltpu.VMEM((comps, total, LANES), F32),
            pltpu.SemaphoreType.DMA((4 + comps,)),
        ],
        compiler_params=pltpu.CompilerParams(vmem_limit_bytes=16 << 20),
        name="relay",
    )(*(
        pltpu.with_memory_space_constraint(x, pltpu.HBM)
        for x in (region_scale, rows, metric, block_map, flags)
    ))


def tensor_kernel(wide_ref, adv_ref, scale_ref, slab_ref, inner_ref, outer_ref, near_ref,
                  far_ref, swap, ny, groups, blocks, keep_ref, send_ref, grad_ref, t0_ref, t1_ref):
    comps, cells, count, _ = wide_ref.shape
    half = keep_ref.shape[1]
    width = count // groups
    tile = min(width, TILE)
    order = test_order(groups)
    block, layer, odd = place()
    raised = layer % 2 == 1
    row = lax.broadcasted_iota(jnp.int32, (cells, LANES), 0)
    lane = lax.broadcasted_iota(jnp.int32, (cells, LANES), 1)
    ends = [layer == 0, layer == groups - 1, block == 0, block == blocks - 1]

    def shift_in(own, before, after, by, axis, first, last, no_before, no_after):
        size = own.shape[axis]
        prev = pltpu.roll(own, by, axis)
        succ = pltpu.roll(own, size - by, axis)
        if before is not None:
            before = jnp.where(no_before, 0.0, pltpu.roll(before, first[1], 0) if first[1] else before)
            after = jnp.where(no_after, 0.0, pltpu.roll(after, last[1], 0) if last[1] else after)
        else:
            before = after = 0.0
        return jnp.where(last[0], after, succ) - jnp.where(first[0], before, prev)

    for c in range(comps):
        for k in range(KS):
            at = pl.ds(k * cells, cells)
            own, inner, outer, near, far = (
                ref[c, at, :].astype(F32)
                for ref in (slab_ref, inner_ref, outer_ref, near_ref, far_ref)
            )
            down, up = jnp.where(raised, inner, outer), jnp.where(raised, outer, inner)
            left, right = jnp.where(odd, near, far), jnp.where(odd, far, near)
            shift_x = ny % cells
            diffs = [
                shift_in(own, down, up, ny % cells, 0, (row < ny, shift_x), (row >= cells - ny, shift_x),
                         ends[0], ends[1]),
                shift_in(own, left, right, 1, 0, (row % ny == 0, (cells - ny + 1) % cells),
                         (row % ny == ny - 1, (ny - 1) % cells), ends[2], ends[3]),
                shift_in(own, None, None, 1, 1, (lane == 0, 0), (lane == LANES - 1, 0), None, None),
            ]
            for d in range(comps):
                grad_ref[(k * comps + d) * comps + c] = diffs[d] * scale_ref[d]

    def build(k, t_ref):
        for q in range(groups):
            base = pl.multiple_of(order[q] * width, width)
            for r in range(cells):
                for i in range(0, width, tile):
                    a = [wide_ref[c, r, pl.ds(base + i, tile), :] for c in range(comps)]
                    for d in range(comps):
                        at = (k * comps + d) * comps
                        g = [grad_ref[at + c, pl.ds(r, 1), :] for c in range(comps)]
                        total = a[0] * g[0]
                        for c in range(1, comps):
                            total = total + a[c] * g[c]
                        top = q * width + i
                        t_ref[d * cells + r, top : top + tile, :] = total.astype(BF16)

    def contract(k, t_ref):
        adv, tested = (
            jnp.concatenate([ref[n] for n in range(ref.shape[0])], axis=1) for ref in (adv_ref, t_ref)
        )
        out = lax.dot_general(
            adv, tested, (((1,), (1,)), ((), ())), preferred_element_type=F32
        )
        keep_ref[k] = out[:half]
        gone = out[half:]
        send_ref[k] = jnp.concatenate(
            [gone[:, s * width : (s + 1) * width] for s in swap], axis=1
        ).astype(BF16)

    build(0, t0_ref)

    def step(n, carry):
        build(2 * n + 1, t1_ref)
        contract(2 * n, t0_ref)
        build(2 * n + 2, t0_ref)
        contract(2 * n + 1, t1_ref)
        return carry

    lax.fori_loop(0, KS // 2 - 1, step, 0)
    build(KS - 1, t1_ref)
    contract(KS - 2, t0_ref)
    contract(KS - 1, t1_ref)


def tensor_parts(wide, adv, scale, slabs, swap, ny, groups, blocks):
    comps, cells, count, _ = wide.shape
    half = count // 2
    return pl.pallas_call(
        lambda *refs: tensor_kernel(*refs[:8], swap, ny, groups, blocks, *refs[8:]),
        out_shape=[vmem((KS, half, count), F32), vmem((KS, half, count), BF16)],
        scratch_shapes=[
            pltpu.VMEM((KS * comps * comps, cells, LANES), F32),
            pltpu.VMEM(adv.shape, BF16),
            pltpu.VMEM(adv.shape, BF16),
        ],
        compiler_params=pltpu.CompilerParams(vmem_limit_bytes=16 << 20),
        name="tensor_parts",
    )(*(inside(x) for x in (wide, adv, scale, *slabs)))


def fold_parts(rows, group, side):
    half = group // 2
    first = side * half
    parts = [r[:, g + first : g + first + half] for r in rows for g in range(0, rows[0].shape[1], group)]
    return parts[0] if len(parts) == 1 else jnp.concatenate(parts, axis=1)


def fold(keep, recv, group):
    count, rows, lanes = keep.shape
    shape = (count // 2, rows, lanes)

    def kernel(keep_ref, recv_ref, own_ref, send_ref):
        for n in range(count // 2):
            pair = [keep_ref[m] + recv_ref[m].astype(F32) for m in (2 * n, 2 * n + 1)]
            own_ref[n] = fold_parts(pair, group, 0)
            send_ref[n] = fold_parts(pair, group, 1).astype(BF16)

    return pl.pallas_call(
        kernel,
        out_shape=[vmem(shape, F32), vmem(shape, BF16)],
        compiler_params=pltpu.CompilerParams(vmem_limit_bytes=4 << 20),
        name="fold",
    )(inside(keep), inside(recv))


def finish(keep, recv, width):
    count, rows, lanes = keep.shape
    pieces = lanes // width

    def kernel(keep_ref, recv_ref, out_ref):
        for n in range(count):
            total = keep_ref[n] + recv_ref[n].astype(F32)
            for q in range(pieces):
                out_ref[n * pieces + q] = total[:, q * width : (q + 1) * width]

    return pl.pallas_call(
        kernel,
        out_shape=jax.ShapeDtypeStruct((KS, rows, width), F32),
        compiler_params=pltpu.CompilerParams(vmem_limit_bytes=4 << 20),
        name="finish",
    )(inside(keep), inside(recv))


def exchange(send, axis, masks):
    count = lax.axis_size(axis)
    return lax.ppermute(send, axis, [(i, i ^ masks[i % 2]) for i in range(count)])


def local(modes, metric, block_map, flags, region_scale):
    groups = lax.axis_size("grp")
    blocks = lax.axis_size("blk")
    comps, count, nx, ny, nz = modes.shape
    cells = nx * ny
    total_cells = nx * groups * ny * blocks * nz
    norm = float(total_cells) ** (-0.5)

    rows = modes.reshape(comps, count * cells, nz)
    slab = rows[:, : KS * cells]
    inner = lax.ppermute(slab, "grp", [(i, i ^ 1) for i in range(groups)])
    outer = lax.ppermute(
        slab, "grp", [(i, i + 1 if i % 2 else i - 1) for i in range(1, groups - 1)]
    )
    turn = [(i + 1) % blocks if i % 2 else (i - 1) % blocks for i in range(blocks)]
    far = lax.ppermute(slab, "blk", list(enumerate(turn)))
    near = lax.ppermute(slab, "blk", [(i, i ^ 1) for i in range(blocks)])

    wide, adv, scale = relay(
        region_scale,
        rows,
        metric.reshape(comps, cells, nz),
        block_map.reshape(cells, nz),
        flags.reshape(cells, nz),
        norm,
        count,
        blocks,
    )
    even_masks, odd_masks = halving_masks(groups, 0)
    even_order = xor_table(even_masks)
    swap = [even_order.index(t) for t in xor_table(odd_masks)]
    keep, send = tensor_parts(
        wide,
        adv,
        scale,
        (slab, inner, outer, near, far),
        swap,
        ny,
        groups,
        blocks,
    )

    recv = exchange(send, "blk", [1, 1])
    for masks in zip(*halving_masks(blocks, 1)):
        total = keep + recv.astype(F32)
        half = total.shape[1] // 2
        keep, send = total[:, :half], total[:, half:].astype(BF16)
        recv = exchange(send, "blk", masks)
    width = count
    for masks in zip(even_masks, odd_masks):
        if width > LANES:
            total = keep + recv.astype(F32)
            half = width // 2
            keep, send = total[..., :half], total[..., half:].astype(BF16)
        else:
            keep, send = fold(keep, recv, width)
        width //= 2
        pairs = [
            (g * blocks + b, (g ^ masks[b % 2]) * blocks + b)
            for g in range(groups)
            for b in range(blocks)
        ]
        recv = lax.ppermute(send, ("grp", "blk"), pairs)
    return jnp.swapaxes(finish(keep, recv, width), 1, 2)


def solution(mesh):
    return jax.shard_map(
        local,
        mesh=mesh,
        in_specs=(
            P(None, None, "grp", "blk", None),
            P(None, "grp", "blk", None),
            P("grp", "blk", None),
            P("grp", "blk", None),
            P(),
        ),
        out_specs=P(None, "grp", "blk"),
        check_vma=False,
    )
```

```python
import jax
import jax.numpy as jnp
import numpy as np
from jax import lax
from jax.experimental import pallas as pl
from jax.experimental.pallas import tpu as pltpu
from jax.sharding import PartitionSpec as P

KS = 8
LANES = 128
TILE = 64
F32 = jnp.float32
BF16 = jnp.bfloat16


def halving_bits(devices, first):
    bits = [1 << b for b in range(first, devices.bit_length() - 1)]
    turn = len(bits) // 2
    return [bits, bits[turn:] + bits[:turn]]


def xor_table(masks):
    table = [0]
    for mask in reversed(masks):
        table = table + [t ^ mask for t in table]
    return table


def row_tables(blocks):
    return [xor_table([bit | 1 for bit in bits]) for bits in halving_bits(blocks, 1)]


def column_tables(groups):
    return [xor_table(bits) for bits in halving_bits(groups, 0)]


def regroup(tables):
    return [tables[0].index(t) for t in tables[1]]


def parity(layer, block):
    value = layer ^ block
    for shift in (8, 4, 2, 1):
        value = value ^ (value >> shift)
    return value & 1


def place():
    block, layer = lax.axis_index("blk"), lax.axis_index("grp")
    return block, layer, parity(layer, block) == 1


def ordered(base, tables, flag):
    return [base ^ (e if e == o else jnp.where(flag, o, e)) for e, o in zip(*tables)]


def vmem(shape, dtype):
    return pltpu.VMEM(shape, dtype)


def inside(x):
    return pltpu.with_memory_space_constraint(x, pltpu.VMEM)


def relay_kernel(region_in, rows_in, metric_in, map_in, flag_in, norm, blocks, wide_ref, adv_ref,
                 scale_ref, region_ref, rows_ref, metric_ref, map_ref, flag_ref, flat_ref, sem):
    comps, cells, count, _ = wide_ref.shape
    width = count // blocks
    pairs = [(region_in, region_ref), (metric_in, metric_ref), (map_in, map_ref), (flag_in, flag_ref)]
    pairs += [(rows_in.at[c], rows_ref.at[c]) for c in range(comps)]
    copies = [pltpu.make_async_copy(a, b, sem.at[n]) for n, (a, b) in enumerate(pairs)]
    for copy in copies[4:] + copies[:4]:
        copy.start()
    block, _, flag = place()
    near = ordered(block, row_tables(blocks), flag)
    order = near + [n ^ 1 for n in near]
    for c in range(comps):
        copies[4 + c].wait()
        flat_ref[c] = rows_ref[c].astype(F32)
        for r in range(cells):
            wide_ref[c, r] = flat_ref[c, pl.ds(r, count, stride=cells), :]
        for p in range(blocks):
            start = pl.multiple_of(order[p] * width, width)
            for r in range(cells):
                part = wide_ref[c, r, pl.ds(start, width), :]
                adv_ref[c * cells + r, p * width : (p + 1) * width, :] = part.astype(BF16)
    for copy in copies[:4]:
        copy.wait()
    scale = jnp.zeros(map_ref.shape, F32)
    for label in range(region_ref.shape[0]):
        scale = jnp.where(map_ref[...] == label, region_ref[label], scale)
    flags = flag_ref[...]
    fluid = jnp.where(flags == 0, 1.0, jnp.where(flags == 1, 0.0, 0.5))
    weight = scale * fluid * norm / (metric_ref[0] * metric_ref[1] * metric_ref[2])
    for d in range(comps):
        scale_ref[d] = 0.5 * metric_ref[d] * weight


def relay(region_scale, rows, metric, block_map, flags, norm, count, blocks):
    comps, total, _ = rows.shape
    cells = total // count
    return pl.pallas_call(
        lambda *refs: relay_kernel(*refs[:5], norm, blocks, *refs[5:]),
        in_specs=[pl.BlockSpec(memory_space=pltpu.HBM)] * 5,
        out_shape=[
            vmem((comps, cells, count, LANES), F32),
            vmem((comps * cells, count, LANES), BF16),
            vmem((comps, cells, LANES), F32),
        ],
        scratch_shapes=[
            pltpu.SMEM(region_scale.shape, F32),
            pltpu.VMEM(rows.shape, BF16),
            pltpu.VMEM(metric.shape, F32),
            pltpu.VMEM(block_map.shape, jnp.int32),
            pltpu.VMEM(flags.shape, jnp.int32),
            pltpu.VMEM((comps, total, LANES), F32),
            pltpu.SemaphoreType.DMA((4 + comps,)),
        ],
        compiler_params=pltpu.CompilerParams(vmem_limit_bytes=16 << 20),
        name="relay",
    )(*(
        pltpu.with_memory_space_constraint(x, pltpu.HBM)
        for x in (region_scale, rows, metric, block_map, flags)
    ))


def tensor_kernel(wide_ref, adv_ref, scale_ref, slab_ref, inner_ref, outer_ref, near_ref,
                  far_ref, swap, row_swap, ny, groups, blocks, keep_ref, send_ref, grad_ref, t0_ref, t1_ref):
    comps, cells, count, _ = wide_ref.shape
    half = keep_ref.shape[1]
    width = count // groups
    tile = min(width, TILE)
    block, layer, flag = place()
    order = ordered(layer, column_tables(groups), flag)
    odd = block % 2 == 1
    raised = layer % 2 == 1
    row = lax.broadcasted_iota(jnp.int32, (cells, LANES), 0)
    lane = lax.broadcasted_iota(jnp.int32, (cells, LANES), 1)
    ends = [layer == 0, layer == groups - 1, block == 0, block == blocks - 1]

    def shift_in(own, before, after, by, axis, first, last, no_before, no_after):
        size = own.shape[axis]
        prev = pltpu.roll(own, by, axis)
        succ = pltpu.roll(own, size - by, axis)
        if before is not None:
            before = jnp.where(no_before, 0.0, pltpu.roll(before, first[1], 0) if first[1] else before)
            after = jnp.where(no_after, 0.0, pltpu.roll(after, last[1], 0) if last[1] else after)
        else:
            before = after = 0.0
        return jnp.where(last[0], after, succ) - jnp.where(first[0], before, prev)

    for c in range(comps):
        for k in range(KS):
            at = pl.ds(k * cells, cells)
            own, inner, outer, near, far = (
                ref[c, at, :].astype(F32)
                for ref in (slab_ref, inner_ref, outer_ref, near_ref, far_ref)
            )
            down, up = jnp.where(raised, inner, outer), jnp.where(raised, outer, inner)
            left, right = jnp.where(odd, near, far), jnp.where(odd, far, near)
            shift_x = ny % cells
            diffs = [
                shift_in(own, down, up, ny % cells, 0, (row < ny, shift_x), (row >= cells - ny, shift_x),
                         ends[0], ends[1]),
                shift_in(own, left, right, 1, 0, (row % ny == 0, (cells - ny + 1) % cells),
                         (row % ny == ny - 1, (ny - 1) % cells), ends[2], ends[3]),
                shift_in(own, None, None, 1, 1, (lane == 0, 0), (lane == LANES - 1, 0), None, None),
            ]
            for d in range(comps):
                grad_ref[(k * comps + d) * comps + c] = diffs[d] * scale_ref[d]

    def build(k, t_ref):
        for q in range(groups):
            base = pl.multiple_of(order[q] * width, width)
            for r in range(cells):
                for i in range(0, width, tile):
                    a = [wide_ref[c, r, pl.ds(base + i, tile), :] for c in range(comps)]
                    for d in range(comps):
                        at = (k * comps + d) * comps
                        g = [grad_ref[at + c, pl.ds(r, 1), :] for c in range(comps)]
                        total = a[0] * g[0]
                        for c in range(1, comps):
                            total = total + a[c] * g[c]
                        top = q * width + i
                        t_ref[d * cells + r, top : top + tile, :] = total.astype(BF16)

    def contract(k, t_ref):
        adv, tested = (
            jnp.concatenate([ref[n] for n in range(ref.shape[0])], axis=1) for ref in (adv_ref, t_ref)
        )
        out = lax.dot_general(
            adv, tested, (((1,), (1,)), ((), ())), preferred_element_type=F32
        )
        low, high = out[:half], out[half:]
        rows = half // len(row_swap)
        low_far, high_far = (
            jnp.concatenate([x[n * rows : (n + 1) * rows] for n in row_swap], axis=0)
            for x in (low, high)
        )

        def columns(even, other, places):
            parts = [
                (other if bin(n).count("1") % 2 else even)[:, n * width : (n + 1) * width]
                for n in places
            ]
            return jnp.concatenate(parts, axis=1)

        keep_ref[k] = columns(low, high, range(groups))
        send_ref[k] = columns(high_far, low_far, swap).astype(BF16)

    build(0, t0_ref)

    def step(n, carry):
        build(2 * n + 1, t1_ref)
        contract(2 * n, t0_ref)
        build(2 * n + 2, t0_ref)
        contract(2 * n + 1, t1_ref)
        return carry

    lax.fori_loop(0, KS // 2 - 1, step, 0)
    build(KS - 1, t1_ref)
    contract(KS - 2, t0_ref)
    contract(KS - 1, t1_ref)


def tensor_parts(wide, adv, scale, slabs, swap, row_swap, ny, groups, blocks):
    comps, cells, count, _ = wide.shape
    half = count // 2
    return pl.pallas_call(
        lambda *refs: tensor_kernel(*refs[:8], swap, row_swap, ny, groups, blocks, *refs[8:]),
        out_shape=[vmem((KS, half, count), F32), vmem((KS, half, count), BF16)],
        scratch_shapes=[
            pltpu.VMEM((KS * comps * comps, cells, LANES), F32),
            pltpu.VMEM(adv.shape, BF16),
            pltpu.VMEM(adv.shape, BF16),
        ],
        compiler_params=pltpu.CompilerParams(vmem_limit_bytes=16 << 20),
        name="tensor_parts",
    )(*(inside(x) for x in (wide, adv, scale, *slabs)))


def fold_parts(rows, group, side):
    half = group // 2
    first = side * half
    parts = [r[:, g + first : g + first + half] for r in rows for g in range(0, rows[0].shape[1], group)]
    return parts[0] if len(parts) == 1 else jnp.concatenate(parts, axis=1)


def fold(keep, recv, group):
    count, rows, lanes = keep.shape
    shape = (count // 2, rows, lanes)

    def kernel(keep_ref, recv_ref, own_ref, send_ref):
        for n in range(count // 2):
            pair = [keep_ref[m] + recv_ref[m].astype(F32) for m in (2 * n, 2 * n + 1)]
            own_ref[n] = fold_parts(pair, group, 0)
            send_ref[n] = fold_parts(pair, group, 1).astype(BF16)

    return pl.pallas_call(
        kernel,
        out_shape=[vmem(shape, F32), vmem(shape, BF16)],
        compiler_params=pltpu.CompilerParams(vmem_limit_bytes=4 << 20),
        name="fold",
    )(inside(keep), inside(recv))


def finish(keep, recv, width):
    count, rows, lanes = keep.shape
    pieces = lanes // width

    def kernel(keep_ref, recv_ref, out_ref):
        for n in range(count):
            total = keep_ref[n] + recv_ref[n].astype(F32)
            for q in range(pieces):
                out_ref[n * pieces + q] = total[:, q * width : (q + 1) * width]

    return pl.pallas_call(
        kernel,
        out_shape=jax.ShapeDtypeStruct((KS, rows, width), F32),
        compiler_params=pltpu.CompilerParams(vmem_limit_bytes=4 << 20),
        name="finish",
    )(inside(keep), inside(recv))


def exchange(send, groups, blocks, target):
    pairs = []
    for g in range(groups):
        for b in range(blocks):
            h, c = target(g, b)
            pairs.append((g * blocks + b, h * blocks + c))
    return lax.ppermute(send, ("grp", "blk"), pairs)


def local(modes, metric, block_map, flags, region_scale):
    groups = lax.axis_size("grp")
    blocks = lax.axis_size("blk")
    comps, count, nx, ny, nz = modes.shape
    cells = nx * ny
    total_cells = nx * groups * ny * blocks * nz
    norm = float(total_cells) ** (-0.5)

    rows = modes.reshape(comps, count * cells, nz)
    slab = rows[:, : KS * cells]

    def outer_of(g, b):
        return (g + 1 if g % 2 else g - 1, b) if 0 < g < groups - 1 else (g, b ^ 1)

    def far_of(g, b):
        return g, (b + 1 if b % 2 else b - 1) % blocks

    inner = exchange(slab, groups, blocks, lambda g, b: (g ^ 1, b))
    outer = exchange(slab, groups, blocks, outer_of)
    far = exchange(slab, groups, blocks, far_of)
    near = exchange(slab, groups, blocks, lambda g, b: (g, b ^ 1))

    wide, adv, scale = relay(
        region_scale,
        rows,
        metric.reshape(comps, cells, nz),
        block_map.reshape(cells, nz),
        flags.reshape(cells, nz),
        norm,
        count,
        blocks,
    )
    keep, send = tensor_parts(
        wide,
        adv,
        scale,
        (slab, inner, outer, near, far),
        regroup(column_tables(groups)),
        regroup(row_tables(blocks)),
        ny,
        groups,
        blocks,
    )

    recv = exchange(send, groups, blocks, lambda g, b: (g, b ^ 1))
    for bits in zip(*halving_bits(blocks, 1)):
        total = keep + recv.astype(F32)
        half = total.shape[1] // 2
        keep, send = total[:, :half], total[:, half:].astype(BF16)
        recv = exchange(send, groups, blocks, lambda g, b: (g, b ^ bits[parity(g, b)] ^ 1))
    width = count
    for bits in zip(*halving_bits(groups, 0)):
        if width > LANES:
            total = keep + recv.astype(F32)
            half = width // 2
            keep, send = total[..., :half], total[..., half:].astype(BF16)
        else:
            keep, send = fold(keep, recv, width)
        width //= 2
        recv = exchange(send, groups, blocks, lambda g, b: (g ^ bits[parity(g, b)], b ^ 1))
    return jnp.swapaxes(finish(keep, recv, width), 1, 2)


def solution(mesh):
    return jax.shard_map(
        local,
        mesh=mesh,
        in_specs=(
            P(None, None, "grp", "blk", None),
            P(None, "grp", "blk", None),
            P("grp", "blk", None),
            P("grp", "blk", None),
            P(),
        ),
        out_specs=P(None, "grp", "blk"),
        check_vma=False,
    )
```

```python
import jax
import jax.numpy as jnp
from jax import lax
from jax.experimental import pallas as pl
from jax.experimental.pallas import tpu as pltpu
from jax.sharding import PartitionSpec as P


KS = 8
LANES = 128
TILE = 64
F32 = jnp.float32
BF16 = jnp.bfloat16


def halving_bits(devices, first):
    bits = [1 << b for b in range(first, devices.bit_length() - 1)]
    turn = len(bits) // 2
    return [bits, bits[turn:] + bits[:turn]]


def xor_table(masks):
    table = [0]
    for mask in reversed(masks):
        table = table + [t ^ mask for t in table]
    return table


def row_tables(blocks):
    return [xor_table([bit | 1 for bit in bits]) for bits in halving_bits(blocks, 1)]


def column_tables(groups):
    return [xor_table(bits) for bits in halving_bits(groups, 0)]


def regroup(tables):
    return [tables[0].index(t) for t in tables[1]]


def parity(layer, block):
    value = layer ^ block
    for shift in (8, 4, 2, 1):
        value = value ^ (value >> shift)
    return value & 1


def place():
    block, layer = lax.axis_index("blk"), lax.axis_index("grp")
    return block, layer, parity(layer, block) == 1


def ordered(base, tables, flag):
    return [base ^ (e if e == o else jnp.where(flag, o, e)) for e, o in zip(*tables)]


def vmem(shape, dtype):
    return pltpu.VMEM(shape, dtype)


def inside(x):
    return pltpu.with_memory_space_constraint(x, pltpu.VMEM)


def relay_kernel(region_in, rows_in, metric_in, map_in, flag_in, norm, blocks, wide_ref, adv_ref,
                 scale_ref, region_ref, rows_ref, metric_ref, map_ref, flag_ref, flat_ref, sem):
    comps, cells, count, _ = wide_ref.shape
    width = count // blocks
    pairs = [(region_in, region_ref), (metric_in, metric_ref), (map_in, map_ref), (flag_in, flag_ref)]
    pairs += [(rows_in.at[c], rows_ref.at[c]) for c in range(comps)]
    copies = [pltpu.make_async_copy(a, b, sem.at[n]) for n, (a, b) in enumerate(pairs)]
    for copy in copies[4:] + copies[:4]:
        copy.start()
    block, _, flag = place()
    near = ordered(block, row_tables(blocks), flag)
    order = near + [n ^ 1 for n in near]
    for c in range(comps):
        copies[4 + c].wait()
        flat_ref[c] = rows_ref[c].astype(F32)
        for r in range(cells):
            wide_ref[c, r] = flat_ref[c, pl.ds(r, count, stride=cells), :]
        for p in range(blocks):
            start = pl.multiple_of(order[p] * width, width)
            for r in range(cells):
                part = wide_ref[c, r, pl.ds(start, width), :]
                adv_ref[c * cells + r, p * width : (p + 1) * width, :] = part.astype(BF16)
    for copy in copies[:4]:
        copy.wait()
    scale = jnp.zeros(map_ref.shape, F32)
    for label in range(region_ref.shape[0]):
        scale = jnp.where(map_ref[...] == label, region_ref[label], scale)
    flags = flag_ref[...]
    fluid = jnp.where(flags == 0, 1.0, jnp.where(flags == 1, 0.0, 0.5))
    weight = scale * fluid * norm / (metric_ref[0] * metric_ref[1] * metric_ref[2])
    for d in range(comps):
        scale_ref[d] = 0.5 * metric_ref[d] * weight


def relay(region_scale, rows, metric, block_map, flags, norm, count, blocks):
    comps, total, _ = rows.shape
    cells = total // count
    return pl.pallas_call(
        lambda *refs: relay_kernel(*refs[:5], norm, blocks, *refs[5:]),
        in_specs=[pl.BlockSpec(memory_space=pltpu.HBM)] * 5,
        out_shape=[
            vmem((comps, cells, count, LANES), F32),
            vmem((comps * cells, count, LANES), BF16),
            vmem((comps, cells, LANES), F32),
        ],
        scratch_shapes=[
            pltpu.SMEM(region_scale.shape, F32),
            pltpu.VMEM(rows.shape, BF16),
            pltpu.VMEM(metric.shape, F32),
            pltpu.VMEM(block_map.shape, jnp.int32),
            pltpu.VMEM(flags.shape, jnp.int32),
            pltpu.VMEM((comps, total, LANES), F32),
            pltpu.SemaphoreType.DMA((4 + comps,)),
        ],
        compiler_params=pltpu.CompilerParams(vmem_limit_bytes=16 << 20),
        name="relay",
    )(*(
        pltpu.with_memory_space_constraint(x, pltpu.HBM)
        for x in (region_scale, rows, metric, block_map, flags)
    ))


def gradients(scale_ref, slab_ref, inner_ref, outer_ref, near_ref, far_ref, ny, groups, blocks, grad_ref):
    comps, cells, _ = scale_ref.shape
    block, layer, _ = place()
    odd = block % 2 == 1
    raised = layer % 2 == 1
    row = lax.broadcasted_iota(jnp.int32, (cells, LANES), 0)
    lane = lax.broadcasted_iota(jnp.int32, (cells, LANES), 1)
    ends = [layer == 0, layer == groups - 1, block == 0, block == blocks - 1]

    def shift_in(own, before, after, by, axis, first, last, no_before, no_after):
        size = own.shape[axis]
        prev = pltpu.roll(own, by, axis)
        succ = pltpu.roll(own, size - by, axis)
        if before is not None:
            before = jnp.where(no_before, 0.0, pltpu.roll(before, first[1], 0) if first[1] else before)
            after = jnp.where(no_after, 0.0, pltpu.roll(after, last[1], 0) if last[1] else after)
        else:
            before = after = 0.0
        return jnp.where(last[0], after, succ) - jnp.where(first[0], before, prev)

    for c in range(comps):
        for k in range(KS):
            at = pl.ds(k * cells, cells)
            own, inner, outer, near, far = (
                ref[c, at, :].astype(F32)
                for ref in (slab_ref, inner_ref, outer_ref, near_ref, far_ref)
            )
            down, up = jnp.where(raised, inner, outer), jnp.where(raised, outer, inner)
            left, right = jnp.where(odd, near, far), jnp.where(odd, far, near)
            shift_x = ny % cells
            diffs = [
                shift_in(own, down, up, ny % cells, 0, (row < ny, shift_x), (row >= cells - ny, shift_x),
                         ends[0], ends[1]),
                shift_in(own, left, right, 1, 0, (row % ny == 0, (cells - ny + 1) % cells),
                         (row % ny == ny - 1, (ny - 1) % cells), ends[2], ends[3]),
                shift_in(own, None, None, 1, 1, (lane == 0, 0), (lane == LANES - 1, 0), None, None),
            ]
            for d in range(comps):
                grad_ref[(k * comps + d) * comps + c] = diffs[d] * scale_ref[d]


def tensor_kernel(wide_ref, adv_ref, grad_ref, swap, row_swap, groups, keep_ref, send_ref, t0_ref, t1_ref, first):
    comps, cells, count, _ = wide_ref.shape
    half = keep_ref.shape[1]
    modes = keep_ref.shape[0]
    width = count // groups
    tile = min(width, TILE)
    _, layer, flag = place()
    order = ordered(layer, column_tables(groups), flag)

    def build(k, t_ref):
        for q in range(groups):
            base = pl.multiple_of(order[q] * width, width)
            for r in range(cells):
                for i in range(0, width, tile):
                    a = [wide_ref[c, r, pl.ds(base + i, tile), :] for c in range(comps)]
                    for d in range(comps):
                        at = ((first + k) * comps + d) * comps
                        g = [grad_ref[at + c, pl.ds(r, 1), :] for c in range(comps)]
                        total = a[0] * g[0]
                        for c in range(1, comps):
                            total = total + a[c] * g[c]
                        top = q * width + i
                        t_ref[d * cells + r, top : top + tile, :] = total.astype(BF16)

    def contract(k, t_ref):
        adv, tested = (
            jnp.concatenate([ref[n] for n in range(ref.shape[0])], axis=1) for ref in (adv_ref, t_ref)
        )
        out = lax.dot_general(
            adv, tested, (((1,), (1,)), ((), ())), preferred_element_type=F32
        )
        low, high = out[:half], out[half:]
        rows = half // len(row_swap)
        low_far, high_far = (
            jnp.concatenate([x[n * rows : (n + 1) * rows] for n in row_swap], axis=0)
            for x in (low, high)
        )

        def columns(even, other, places):
            parts = [
                (other if bin(n).count("1") % 2 else even)[:, n * width : (n + 1) * width]
                for n in places
            ]
            return jnp.concatenate(parts, axis=1)

        keep_ref[k] = columns(low, high, range(groups))
        send_ref[k] = columns(high_far, low_far, swap).astype(BF16)

    build(0, t0_ref)

    def step(n, carry):
        build(2 * n + 1, t1_ref)
        contract(2 * n, t0_ref)
        build(2 * n + 2, t0_ref)
        contract(2 * n + 1, t1_ref)
        return carry

    lax.fori_loop(0, modes // 2 - 1, step, 0)
    build(modes - 1, t1_ref)
    contract(modes - 2, t0_ref)
    contract(modes - 1, t1_ref)


def tensor_parts(wide, adv, first, modes, swaps, groups, blocks, grads=None, halo=None):
    comps, cells, count, _ = wide.shape
    half = count // 2
    outs = [vmem((modes, half, count), F32), vmem((modes, half, count), BF16)]
    scratch = [pltpu.VMEM(adv.shape, BF16), pltpu.VMEM(adv.shape, BF16)]
    if grads is None:
        scale, slabs, ny = halo
        outs.append(vmem((KS * comps * comps, cells, LANES), F32))

        def kernel(wide_ref, adv_ref, *refs):
            keep_ref, send_ref, grad_ref, t0_ref, t1_ref = refs[6:]
            gradients(*refs[:6], ny, groups, blocks, grad_ref)
            tensor_kernel(
                wide_ref, adv_ref, grad_ref, *swaps, groups, keep_ref, send_ref, t0_ref, t1_ref, first
            )

        operands = (wide, adv, scale, *slabs)
    else:

        def kernel(wide_ref, adv_ref, grad_ref, *refs):
            tensor_kernel(wide_ref, adv_ref, grad_ref, *swaps, groups, *refs, first)

        operands = (wide, adv, grads)
    return pl.pallas_call(
        kernel,
        out_shape=outs,
        scratch_shapes=scratch,
        compiler_params=pltpu.CompilerParams(vmem_limit_bytes=16 << 20),
        name="tensor_parts",
    )(*(inside(x) for x in operands))


def fold_parts(rows, group, side):
    half = group // 2
    first = side * half
    parts = [r[:, g + first : g + first + half] for r in rows for g in range(0, rows[0].shape[1], group)]
    return parts[0] if len(parts) == 1 else jnp.concatenate(parts, axis=1)


def fold(keep, recv, group):
    count, rows, lanes = keep.shape
    shape = (count // 2, rows, lanes)

    def kernel(keep_ref, recv_ref, own_ref, send_ref):
        for n in range(count // 2):
            pair = [keep_ref[m] + recv_ref[m].astype(F32) for m in (2 * n, 2 * n + 1)]
            own_ref[n] = fold_parts(pair, group, 0)
            send_ref[n] = fold_parts(pair, group, 1).astype(BF16)

    return pl.pallas_call(
        kernel,
        out_shape=[vmem(shape, F32), vmem(shape, BF16)],
        compiler_params=pltpu.CompilerParams(vmem_limit_bytes=4 << 20),
        name="fold",
    )(inside(keep), inside(recv))


def finish(keep, recv, width):
    count, rows, lanes = keep.shape
    pieces = lanes // width

    def kernel(keep_ref, recv_ref, out_ref):
        for n in range(count):
            total = keep_ref[n] + recv_ref[n].astype(F32)
            for q in range(pieces):
                out_ref[n * pieces + q] = total[:, q * width : (q + 1) * width]

    return pl.pallas_call(
        kernel,
        out_shape=jax.ShapeDtypeStruct((KS, rows, width), F32),
        compiler_params=pltpu.CompilerParams(vmem_limit_bytes=4 << 20),
        name="finish",
    )(inside(keep), inside(recv))


def exchange(send, groups, blocks, target):
    pairs = []
    for g in range(groups):
        for b in range(blocks):
            h, c = target(g, b)
            pairs.append((g * blocks + b, h * blocks + c))
    return lax.ppermute(send, ("grp", "blk"), pairs)


def local(modes, metric, block_map, flags, region_scale):
    groups = lax.axis_size("grp")
    blocks = lax.axis_size("blk")
    comps, count, nx, ny, nz = modes.shape
    cells = nx * ny
    total_cells = nx * groups * ny * blocks * nz
    norm = float(total_cells) ** (-0.5)

    rows = modes.reshape(comps, count * cells, nz)
    slab = rows[:, : KS * cells]

    def outer_of(g, b):
        return (g + 1 if g % 2 else g - 1, b) if 0 < g < groups - 1 else (g, b ^ 1)

    def far_of(g, b):
        return (g, b + 1 if b % 2 else b - 1) if 0 < b < blocks - 1 else (g ^ 1, b)

    outer = exchange(slab, groups, blocks, outer_of)
    inner = exchange(slab, groups, blocks, lambda g, b: (g ^ 1, b))
    far = exchange(slab, groups, blocks, far_of)
    near = exchange(slab, groups, blocks, lambda g, b: (g, b ^ 1))

    wide, adv, scale = relay(
        region_scale,
        rows,
        metric.reshape(comps, cells, nz),
        block_map.reshape(cells, nz),
        flags.reshape(cells, nz),
        norm,
        count,
        blocks,
    )
    swaps = regroup(column_tables(groups)), regroup(row_tables(blocks))
    lead = KS - 2
    keep, send, grads = tensor_parts(
        wide, adv, 0, lead, swaps, groups, blocks, halo=(scale, (slab, inner, outer, near, far), ny)
    )

    def other_core(g, b):
        return g, b ^ 1

    parts = [(keep, exchange(send, groups, blocks, other_core))]
    keep, send = tensor_parts(wide, adv, lead, KS - lead, swaps, groups, blocks, grads=grads)
    parts.append((keep, exchange(send, groups, blocks, other_core)))
    for n, bits in enumerate(zip(*halving_bits(blocks, 1))):
        def step(g, b):
            return g, b ^ bits[parity(g, b)] ^ 1

        totals = []
        for keep, recv in parts:
            totals.append(keep + recv.astype(F32))
        if n == 1:
            totals = [jnp.concatenate(totals)]
        half = totals[0].shape[1] // 2
        parts = []
        for total in totals:
            recv = exchange(total[:, half:].astype(BF16), groups, blocks, step)
            parts.append((total[:, :half], recv))
    keep, recv = parts[0]
    width = count
    for bits in zip(*halving_bits(groups, 0)):
        if width > LANES:
            total = keep + recv.astype(F32)
            half = width // 2
            keep, send = total[..., :half], total[..., half:].astype(BF16)
        else:
            keep, send = fold(keep, recv, width)
        width //= 2
        recv = exchange(send, groups, blocks, lambda g, b: (g ^ bits[parity(g, b)], b ^ 1))
    return jnp.swapaxes(finish(keep, recv, width), 1, 2)


def solution(mesh):
    return jax.shard_map(
        local,
        mesh=mesh,
        in_specs=(
            P(None, None, "grp", "blk", None),
            P(None, "grp", "blk", None),
            P("grp", "blk", None),
            P("grp", "blk", None),
            P(),
        ),
        out_specs=P(None, "grp", "blk"),
        check_vma=False,
    )
```
